32 devices in a mesh: row: 8 (over z, x), col: 4 (over y, core).
Axes of the slice: x: 2, y: 2, z: 4, core: 2. Of those that a mesh axis runs over, the one named last changes fastest.
Arguments:
- charges: float32 [32768], P(('row', 'col')), may hold values from -0.5 to 1.5
- structure_id: int32 [32768], P(('row', 'col')), may hold values from 0 to 255, as said below
- live_count: int32 [32], P(('row', 'col')), may hold values from 512 to 1024, as said below
- cell_index: int32 [3, 32768], P(None, ('row', 'col')), may hold values from 0 to 255, as said below
- fraction: float32 [3, 32768], P(None, ('row', 'col')), may hold values from 0 to 1
- influence: float32 [256, 64, 64], P('col', 'row'), may hold values from 0.1 to 10
Outputs:
- forces: float32 [3, 32768], P(None, ('row', 'col'))
- atom_energy: float32 [32768], P(('row', 'col'))
The draws below stay inside these ranges and needn't reach their ends.
Inputs may be any that keep to these rules, and one draw needn't show every extreme that they name: `structure_id`: devices are numbered row-major over (row, col). Slots 0 to 7 of device d are live and belong to fragments d * 8 to d * 8 + 7, so every fragment has a live atom; every other slot names a fragment of its own device, of one of the four devices beside it along row or col (wrapping around), or of the device whose number is d plus half the number of devices (wrapping around). Device d's live atoms are its first live_count[d] slots; the count reaches 1024 on some device in every draw. `cell_index`: the atom slots of the device at (row r, col c) lie in its mesh block: first index from r * 8 to r * 8 + 7, second from c * 16 to c * 16 + 15; the third is anywhere.
All inputs are finite; a program needn't handle non-finite values.
Results may differ from the reference program's by a relative error of at most 0.000065.
Values sent between devices are 32-bit elements; how exact they have to be, the bound alone decides.
A program may use at most 64 MiB of HBM per device.

```python
import math
import jax
import jax.numpy as jnp
from jax import lax

CX = 8
CY = 16
NZ = 256
ATOM_DEV = 1024
S_DEV = 8
NX = 64
NY = 64
ATOMS = 32768
STRUCTS = 256
N_ROW = 8
N_COL = 4
DEVICES = 32


def draw_structure_id(key, part):
    key_side, key_pick = jax.random.split(jax.random.fold_in(key, 5))
    atom_slot = lax.iota(jnp.int32, ATOMS)
    device = atom_slot // ATOM_DEV
    within = atom_slot % ATOM_DEV
    row_place = device // N_COL
    col_place = device % N_COL
    side = jax.random.randint(key_side, (ATOMS,), 0, 6)
    row_step = jnp.where(side == 1, 1, jnp.where(side == 2, -1, 0))
    col_step = jnp.where(side == 3, 1, jnp.where(side == 4, -1, 0))
    owner = (row_place + row_step + N_ROW) % N_ROW * N_COL + (col_place + col_step + N_COL) % N_COL
    far_owner = (device + DEVICES // 2) % DEVICES
    owner = jnp.where(side == 5, far_owner, owner)
    nearby = owner * S_DEV + jax.random.randint(key_pick, (ATOMS,), 0, S_DEV)
    return jnp.where(within < S_DEV, device * S_DEV + within, nearby).astype(jnp.int32)


def draw_live_count(key, part):
    key_counts, key_fullest = jax.random.split(jax.random.fold_in(key, 7))
    least_live = max(S_DEV, ATOM_DEV // 2)
    counts = jax.random.randint(key_counts, (DEVICES,), least_live, ATOM_DEV + 1)
    fullest = jax.random.randint(key_fullest, (), 0, DEVICES)
    return jnp.where(lax.iota(jnp.int32, DEVICES) == fullest, ATOM_DEV, counts).astype(jnp.int32)


def draw_cell_index(key, part):
    key_x, key_y, key_z = jax.random.split(jax.random.fold_in(key, 11), 3)
    atom_slot = lax.iota(jnp.int32, ATOMS)
    device = atom_slot // ATOM_DEV
    row_place = device // N_COL
    col_place = device % N_COL
    cell_x = row_place * CX + jax.random.randint(key_x, (ATOMS,), 0, CX)
    cell_y = col_place * CY + jax.random.randint(key_y, (ATOMS,), 0, CY)
    cell_z = jax.random.randint(key_z, (ATOMS,), 0, NZ)
    return jnp.stack([cell_x, cell_y, cell_z]).astype(jnp.int32)


def block_levels(key, dims, shards, smallest, high):
    def one(dim, shards_of):
        draws = jax.random.uniform(jax.random.fold_in(jax.random.fold_in(key, 6), dim), (shards_of,), jnp.float32, smallest / len(shards), high / len(shards))
        return jnp.repeat(jnp.exp(draws), dims[dim] // shards_of).reshape((-1,) + (1,) * (len(dims) - dim - 1))

    level = one(*shards[0])
    for cut in shards[1:]:
        level = level * one(*cut)
    return level


def setup_inputs(seed: int = 0) -> dict:
    key_of = jax.random.split(jax.random.key(seed), 7)
    return {
        "charges": jnp.clip(-0.5 + 2.0 * jax.random.uniform(key_of[0], (ATOMS,), jnp.float32) ** block_levels(key_of[0], (ATOMS,), ((0, 32),), -0.2, 0.2), -0.5, 1.5),
        "structure_id": draw_structure_id(jax.random.fold_in(key_of[6], 71), 0),
        "live_count": draw_live_count(jax.random.fold_in(key_of[6], 71), 0),
        "cell_index": draw_cell_index(jax.random.fold_in(key_of[6], 71), 0),
        "fraction": jnp.clip(1.0 * jax.random.uniform(key_of[4], (3, ATOMS), jnp.float32) ** block_levels(key_of[4], (3, ATOMS), ((1, 32),), -0.2, 0.2), 0.0, 1.0),
        "influence": jnp.clip(jnp.exp(math.log(10.0) - 4.6051702 * jax.random.uniform(key_of[5], (NZ, NY, NX), jnp.float32) ** block_levels(key_of[5], (NZ, NY, NX), ((0, 4), (1, 8)), -0.2, 0.2)), 0.1, 10.0),
    }


def spline_weights(fraction):
    remain = 1.0 - fraction
    square = fraction * fraction
    cubic_term = square * fraction
    values = [remain * remain * remain / 6.0, (3.0 * cubic_term - 6.0 * square + 4.0) / 6.0,
              (-3.0 * cubic_term + 3.0 * square + 3.0 * fraction + 1.0) / 6.0, cubic_term / 6.0]
    slopes = [-0.5 * remain * remain, 0.5 * (3.0 * square - 4.0 * fraction),
              0.5 * (-3.0 * square + 2.0 * fraction + 1.0), 0.5 * square]
    return values, slopes


def reference(charges, structure_id, live_count, cell_index, fraction, influence):
    atom_slot = jnp.arange(ATOMS, dtype=jnp.int32)
    live = ((atom_slot % ATOM_DEV) < live_count[atom_slot // ATOM_DEV]).astype(jnp.float32)
    totals = jax.ops.segment_sum(charges * live, structure_id, num_segments=STRUCTS)
    counts = jax.ops.segment_sum(live, structure_id, num_segments=STRUCTS)
    neutral = (charges - (totals / counts)[structure_id]) * live
    wx_val, wx_slope = spline_weights(fraction[0])
    wy_val, wy_slope = spline_weights(fraction[1])
    wz_val, wz_slope = spline_weights(fraction[2])
    density = jnp.zeros((NX, NY, NZ), jnp.float32)
    for first in range(4):
        cell_x = (cell_index[0] + first) % NX
        for second in range(4):
            cell_y = (cell_index[1] + second) % NY
            partial_xy = neutral * wx_val[first] * wy_val[second]
            for third in range(4):
                cell_z = (cell_index[2] + third) % NZ
                density = density.at[cell_x, cell_y, cell_z].add(partial_xy * wz_val[third])
    spectrum = jnp.fft.fftn(density)
    kernel = jnp.transpose(influence, (2, 1, 0))
    potential = jnp.real(jnp.fft.ifftn(spectrum * kernel))
    value = jnp.zeros_like(charges)
    grad_x = jnp.zeros_like(charges)
    grad_y = jnp.zeros_like(charges)
    grad_z = jnp.zeros_like(charges)
    for first in range(4):
        cell_x = (cell_index[0] + first) % NX
        for second in range(4):
            cell_y = (cell_index[1] + second) % NY
            for third in range(4):
                cell_z = (cell_index[2] + third) % NZ
                sample = potential[cell_x, cell_y, cell_z]
                value = value + wx_val[first] * wy_val[second] * wz_val[third] * sample
                grad_x = grad_x + wx_slope[first] * wy_val[second] * wz_val[third] * sample
                grad_y = grad_y + wx_val[first] * wy_slope[second] * wz_val[third] * sample
                grad_z = grad_z + wx_val[first] * wy_val[second] * wz_slope[third] * sample
    atom_energy = 0.5 * neutral * value
    forces = -neutral[None, :] * jnp.stack([grad_x, grad_y, grad_z])
    return forces, atom_energy
```

```python
import math

import functools

import jax
import jax.numpy as jnp
import numpy as np
from jax import lax
from jax.experimental import pallas as pl
from jax.experimental.pallas import tpu as pltpu
from jax.sharding import PartitionSpec as P

CX = 8
CY = 16
NZ = 256
S_DEV = 8


highest = lax.Precision.HIGHEST


def passed_along(block, axis, distance):
    devices = range(lax.axis_size(axis))
    route = [((i - distance) % len(devices), i) for i in devices]
    return lax.ppermute(block, axis, route)


def spline_weights(fraction):
    remain = 1.0 - fraction
    square = fraction * fraction
    cubic_term = square * fraction
    values = [
        remain * remain * remain / 6.0,
        (3.0 * cubic_term - 6.0 * square + 4.0) / 6.0,
        (-3.0 * cubic_term + 3.0 * square + 3.0 * fraction + 1.0) / 6.0,
        cubic_term / 6.0,
    ]
    slopes = [
        -0.5 * remain * remain,
        0.5 * (3.0 * square - 4.0 * fraction),
        0.5 * (-3.0 * square + 2.0 * fraction + 1.0),
        0.5 * square,
    ]
    return (values, slopes)


def place_weights(weights, local, width, period):
    columns = lax.broadcasted_iota(jnp.int32, (local.shape[0], width), 1)
    result = jnp.zeros((local.shape[0], width), jnp.float32)
    for offset in range(4):
        target = (local + offset) % period
        result = result + jnp.where(columns == target[:, None], weights[offset][:, None], 0.0)
    return result


def dft_tables(length):
    counter = lax.iota(jnp.int32, length)
    product = counter[:, None] * counter[None, :] % length
    angle = 2.0 * math.pi / length * product.astype(jnp.float32)
    return (jnp.cos(angle), jnp.sin(angle))


def rotate_pair(real_part, imag_part, pattern, cosine, sine, direction):
    real_cos = jnp.einsum(pattern, real_part, cosine, precision=highest)
    real_sin = jnp.einsum(pattern, real_part, sine, precision=highest)
    imag_cos = jnp.einsum(pattern, imag_part, cosine, precision=highest)
    imag_sin = jnp.einsum(pattern, imag_part, sine, precision=highest)
    return (real_cos - direction * imag_sin, imag_cos + direction * real_sin)


def body(charges, structure_id, live_count, cell_index, fraction, influence):
    atom_total = charges.shape[0]
    row_count = lax.axis_size("row")
    col_count = lax.axis_size("col")
    mesh_x = CX * row_count
    mesh_y = CY * col_count
    structures = S_DEV * row_count * col_count
    local_x = cell_index[0] - lax.axis_index("row") * CX
    local_y = cell_index[1] - lax.axis_index("col") * CY
    live = (lax.iota(jnp.int32, atom_total) < live_count[0]).astype(jnp.float32)
    wx_val, wx_slope = spline_weights(fraction[0])
    wy_val, wy_slope = spline_weights(fraction[1])
    wz_val, wz_slope = spline_weights(fraction[2])
    big_period = 4 * (CX + CY + 8)
    x_rows = place_weights(wx_val, local_x, CX + 3, big_period)
    x_slope_rows = place_weights(wx_slope, local_x, CX + 3, big_period)
    y_rows = place_weights(wy_val, local_y, CY + 3, big_period)
    y_slope_rows = place_weights(wy_slope, local_y, CY + 3, big_period)
    z_rows = place_weights(wz_val, cell_index[2], NZ, NZ)
    z_slope_rows = place_weights(wz_slope, cell_index[2], NZ, NZ)
    plane = (y_rows[:, :, None] * x_rows[:, None, :]).reshape(atom_total, -1)
    charge_sums = jax.ops.segment_sum(charges * live, structure_id, num_segments=structures)
    live_sums = jax.ops.segment_sum(live, structure_id, num_segments=structures)
    totals, counts = lax.psum((charge_sums, live_sums), ("row", "col"))
    neutral = (charges - jnp.take(totals / counts, structure_id)) * live
    spread_grid = lax.dot_general(
        plane,
        neutral[:, None] * z_rows,
        (((0,), (0,)), ((), ())),
        precision=highest,
        preferred_element_type=jnp.float32,
    )
    extended = spread_grid.reshape(CY + 3, CX + 3, NZ)
    spill_x = passed_along(extended[:, CX:, :], "row", 1)
    extended = extended[:, :CX, :].at[:, :3, :].add(spill_x)
    spill_y = passed_along(extended[CY:], "col", 1)
    density = extended[:CY].at[:3].add(spill_y)
    cos_z, sin_z = dft_tables(NZ)
    cos_y, sin_y = dft_tables(mesh_y)
    cos_x, sin_x = dft_tables(mesh_x)
    real_z = jnp.einsum("yxz,zk->kxy", density, cos_z, precision=highest)
    imag_z = -jnp.einsum("yxz,zk->kxy", density, sin_z, precision=highest)
    columns = lax.all_to_all(
        jnp.stack([real_z, imag_z]), "col", split_axis=1, concat_axis=3, tiled=True
    )
    real_y, imag_y = rotate_pair(columns[0], columns[1], "zxy,yk->zkx", cos_y, sin_y, -1.0)
    rows = lax.all_to_all(
        jnp.stack([real_y, imag_y]), "row", split_axis=2, concat_axis=3, tiled=True
    )
    real_x, imag_x = rotate_pair(rows[0], rows[1], "zyx,xk->zyk", cos_x, sin_x, -1.0)
    scale = influence / float(mesh_x * mesh_y * NZ)
    real_x = real_x * scale
    imag_x = imag_x * scale
    back_x, back_x_imag = rotate_pair(real_x, imag_x, "zyk,kx->zyx", cos_x, sin_x, 1.0)
    returned = lax.all_to_all(
        jnp.stack([back_x, back_x_imag]), "row", split_axis=3, concat_axis=2, tiled=True
    )
    back_y, back_y_imag = rotate_pair(returned[0], returned[1], "zkx,ky->zxy", cos_y, sin_y, 1.0)
    whole_z = lax.all_to_all(
        jnp.stack([back_y, back_y_imag]), "col", split_axis=3, concat_axis=1, tiled=True
    )
    potential = jnp.einsum("kxy,kz->yxz", whole_z[0], cos_z, precision=highest) - jnp.einsum(
        "kxy,kz->yxz", whole_z[1], sin_z, precision=highest
    )
    upper_x = passed_along(potential[:, :3, :], "row", -1)
    widened = jnp.concatenate([potential, upper_x], axis=1)
    upper_y = passed_along(widened[:3], "col", -1)
    widened = jnp.concatenate([widened, upper_y], axis=0).reshape(-1, NZ)
    sampled = lax.dot_general(
        jnp.concatenate([z_rows, z_slope_rows], axis=0),
        widened,
        (((1,), (1,)), ((), ())),
        precision=highest,
        preferred_element_type=jnp.float32,
    )
    sample_val = sampled[:atom_total]
    sample_slope = sampled[atom_total:]
    plane_dx = (y_rows[:, :, None] * x_slope_rows[:, None, :]).reshape(atom_total, -1)
    plane_dy = (y_slope_rows[:, :, None] * x_rows[:, None, :]).reshape(atom_total, -1)
    value = jnp.sum(plane * sample_val, axis=1)
    grad_x = jnp.sum(plane_dx * sample_val, axis=1)
    grad_y = jnp.sum(plane_dy * sample_val, axis=1)
    grad_z = jnp.sum(plane * sample_slope, axis=1)
    atom_energy = 0.5 * neutral * value
    forces = -neutral[None, :] * jnp.stack([grad_x, grad_y, grad_z])
    return (forces, atom_energy)


EXT_Y = CY + 3
HALO_ROWS = 24
PLANE = 256
LANES = 128
MESH = pl.DeviceIdType.MESH


def plane_cells():
    cells = np.zeros((PLANE, 2), np.int64)
    used = np.zeros((PLANE,), bool)
    for y in range(EXT_Y):
        for x in range(CX):
            cells[y * CX + x] = (x, y)
            used[y * CX + x] = True
    for x in range(3):
        for y in range(EXT_Y):
            cells[EXT_Y * CX + x * HALO_ROWS + y] = (CX + x, y)
            used[EXT_Y * CX + x * HALO_ROWS + y] = True
    return cells, used


def make_plan(rows, cols):
    n = rows * cols
    offsets = [(0, 0), (1, 0), (-1, 0), (0, 1), (0, -1), (rows // 2, 0)]
    distinct = len({(a % rows, b % cols) for a, b in offsets}) == len(offsets)
    if not (
        rows % 2 == 0
        and cols % 2 == 0
        and distinct
        and NZ % (2 * n) == 0
        and (NZ // n) % 8 == 0
        and NZ % (cols * n) == 0
        and (CY * cols) % rows == 0
        and (CY * cols // rows) % cols == 0
        and (NZ // n) * n == PLANE
        and NZ // n // 2 * n == LANES
    ):
        return None
    return (rows, cols, tuple(offsets))


def make_tables(rows, cols):
    n = rows * cols
    half = NZ // n // 2
    slots = 2 * half
    z = np.arange(NZ)
    forward_z = np.zeros((n, 2, half, NZ))
    for p in range(n):
        for j in range(half):
            angle = 2 * np.pi * ((p + n * j) * z % NZ) / NZ
            forward_z[p, 0, j] = np.cos(angle)
            forward_z[p, 1, j] = -np.sin(angle)
    forward_z[0, 1, 0] = 1.0 - 2.0 * (z % 2)
    forward_z = forward_z.reshape(NZ, NZ)

    r, c, m1, k1 = np.meshgrid(
        np.arange(rows), np.arange(cols), np.arange(cols), np.arange(rows), indexing="ij"
    )
    phi = 2 * np.pi * ((k1 * r % rows) / rows + (m1 * c % cols) / cols)
    phi = phi.reshape(n, n)
    cosp, sinp = np.cos(phi), np.sin(phi)
    gather = np.zeros((2, n, 2, half, 2, slots, n))
    for kind in range(2):
        for t in range(slots):
            j, sign = t, 1.0
            if t >= half:
                j, sign = (slots - 1 - t if kind else slots - t), -1.0
            if kind == 0 and t in (0, half):
                part = 0 if t == 0 else 1
                gather[kind, :, part, 0, 0, t] = cosp
                gather[kind, :, part, 0, 1, t] = -sinp
                continue
            gather[kind, :, 0, j, 0, t] = cosp
            gather[kind, :, 1, j, 0, t] = sign * sinp
            gather[kind, :, 0, j, 1, t] = -sinp
            gather[kind, :, 1, j, 1, t] = sign * cosp
    gather = gather.reshape(2, n * 2 * half, 2 * slots * n)

    cells, used = plane_cells()
    x, y = cells[:, 0], cells[:, 1]
    low_m, low_k = (v.reshape(-1) for v in np.meshgrid(np.arange(cols), np.arange(rows), indexing="ij"))
    psi = 2 * np.pi * (
        x[:, None] * low_k[None] / (CX * rows) + y[:, None] * low_m[None] / (CY * cols)
    )
    twiddle = np.stack([np.tile(np.cos(psi), (1, slots)), np.tile(np.sin(psi), (1, slots))])
    high_m, high_k = (v.reshape(-1) for v in np.meshgrid(np.arange(CY), np.arange(CX), indexing="ij"))
    chi = 2 * np.pi * (high_k[:, None] * x[None] % CX / CX + high_m[:, None] * y[None] % CY / CY)
    cosc, sinc = np.cos(chi) * used[None], np.sin(chi) * used[None]
    inner = np.block([[cosc, sinc], [-sinc, cosc]])
    tables = (forward_z, gather, twiddle, inner, inner.T)
    return tuple(np.ascontiguousarray(t).astype(np.float32) for t in tables)


def dot(left, right, contract):
    return lax.dot_general(
        left,
        right,
        ((contract[:1], contract[1:]), ((), ())),
        precision=highest,
        preferred_element_type=jnp.float32,
    )


def pick(distance, weights):
    result = jnp.where(distance == 3, weights[3], 0.0)
    for i in (2, 1, 0):
        result = jnp.where(distance == i, weights[i], result)
    return result


def kernel(
    plan,
    charges_ref, sid_ref, live_ref, cell_ref, frac_ref, influence_ref,
    fz_hbm, gather_hbm, twiddle_hbm, inner_hbm, inner_t_hbm,
    forces_ref, energy_ref,
    fz, gather, twiddle, inner, inner_t,
    z_rows, z_slopes, plane, x_rows, y_rows,
    frag_out, frag_in, mean_out, mean_in,
    kernel_in, field_out, field_in, back_out, back_in, sampled,
    table_sems, frag_send, frag_recv, mean_send, mean_recv,
    inf_send, inf_recv, field_send, field_recv, back_send, back_recv,
):
    rows, cols, offsets = plan
    n = rows * cols
    r, c = lax.axis_index("row"), lax.axis_index("col")
    me = r * cols + c
    atoms = charges_ref.shape[1]

    def coords(p):
        return (p // cols, lax.rem(p, cols))

    barrier = pltpu.get_barrier_semaphore()

    @pl.loop(1, n)
    def _(o):
        pl.semaphore_signal(
            barrier, inc=1, device_id=coords(lax.rem(me + o, n)), device_id_type=MESH
        )

    tables = [
        pltpu.make_async_copy(fz_hbm, fz, table_sems.at[0]),
        pltpu.make_async_copy(gather_hbm.at[jnp.minimum(me, 1)], gather, table_sems.at[1]),
        pltpu.make_async_copy(twiddle_hbm, twiddle, table_sems.at[2]),
        pltpu.make_async_copy(inner_hbm, inner, table_sems.at[3]),
        pltpu.make_async_copy(inner_t_hbm, inner_t, table_sems.at[4]),
    ]
    for table in tables:
        table.start()

    lane = lax.broadcasted_iota(jnp.int32, (1, atoms), 1)
    live = (lane < live_ref[...]).astype(jnp.float32)
    charges = charges_ref[...]
    charged = charges * live
    sid = sid_ref[...]
    within = lax.broadcasted_iota(jnp.int32, (S_DEV, atoms), 0)
    steps = [
        (lax.rem(r + a % rows, rows), lax.rem(c + b % cols, cols)) for a, b in offsets
    ]
    senders = [
        (lax.rem(r + (-a) % rows, rows), lax.rem(c + (-b) % cols, cols)) for a, b in offsets
    ]

    def belongs(o):
        owner = steps[o][0] * cols + steps[o][1]
        return sid == within + owner * S_DEV

    def folded(values):
        total = values[:, :LANES]
        for k in range(1, atoms // LANES):
            total = total + values[:, k * LANES : (k + 1) * LANES]
        return total

    for o in range(len(offsets)):
        mine = belongs(o)
        frag_out[o, :S_DEV] = folded(jnp.where(mine, charged, 0.0))
        frag_out[o, S_DEV:] = folded(jnp.where(mine, live, 0.0))
    pl.semaphore_wait(barrier, n - 1)
    first = [
        pltpu.make_async_remote_copy(
            frag_out.at[o], frag_in.at[o], frag_send.at[o], frag_recv.at[o],
            device_id=steps[o], device_id_type=MESH,
        )
        for o in range(1, len(offsets))
    ]
    for copy in first:
        copy.start()

    wx, vx = spline_weights(frac_ref[0:1, :])
    wy, vy = spline_weights(frac_ref[1:2, :])
    wz, vz = spline_weights(frac_ref[2:3, :])
    cell_z = cell_ref[2:3, :]
    step = 16

    @pl.loop(0, NZ // step)
    def _(b):
        start = pl.multiple_of(b * step, step)
        index = lax.broadcasted_iota(jnp.int32, (step, atoms), 0) + start - cell_z
        distance = jnp.where(index < 0, index + NZ, index)
        z_rows[pl.ds(start, step), :] = pick(distance, wz)
        z_slopes[pl.ds(start, step), :] = pick(distance, vz)

    distance = lax.broadcasted_iota(jnp.int32, (16, atoms), 0) - (cell_ref[0:1, :] - r * CX)
    x_rows[0] = pick(distance, wx)
    x_rows[1] = pick(distance, vx)
    distance = lax.broadcasted_iota(jnp.int32, (HALO_ROWS, atoms), 0) - (
        cell_ref[1:2, :] - c * CY
    )
    y_rows[0] = pick(distance, wy)
    y_rows[1] = pick(distance, vy)

    for copy in first:
        copy.wait()
    total = frag_out[0]
    for o in range(1, len(offsets)):
        total = total + frag_in[o]
    charge_sum = jnp.sum(total[:S_DEV], axis=1, keepdims=True)
    live_sum = jnp.sum(total[S_DEV:], axis=1, keepdims=True)
    own_mean = charge_sum / live_sum
    mean_out[...] = jnp.broadcast_to(own_mean, (S_DEV, LANES))
    second = [
        pltpu.make_async_remote_copy(
            mean_out, mean_in.at[o], mean_send.at[o], mean_recv.at[o],
            device_id=senders[o], device_id_type=MESH,
        )
        for o in range(1, len(offsets))
    ]
    for copy in second:
        copy.start()

    place = c * rows + r

    def inf_copy(o):
        p = lax.rem(me + o, n)
        residue = jnp.where(c < cols // 2, p, lax.rem(n - p, n))
        return pltpu.make_async_remote_copy(
            influence_ref.at[residue], kernel_in.at[place], inf_send.at[o], inf_recv.at[o],
            device_id=coords(p), device_id_type=MESH,
        )

    @pl.loop(1, n)
    def _(o):
        inf_copy(o).start()

    own_inf = pltpu.make_async_copy(
        influence_ref.at[jnp.where(c < cols // 2, me, lax.rem(n - me, n))],
        kernel_in.at[place],
        inf_recv.at[0],
    )
    own_inf.start()

    for copy in second:
        copy.wait()
    mean = jnp.where(belongs(0), own_mean, 0.0)
    for o in range(1, len(offsets)):
        mean = mean + jnp.where(belongs(o), mean_in[o][:, 0:1], 0.0)
    mean = jnp.sum(mean, axis=0, keepdims=True)
    neutral = (charges - mean) * live

    x_charged = x_rows[0, :CX] * neutral
    for y in range(EXT_Y):
        plane[y * CX : (y + 1) * CX, :] = y_rows[0, y : y + 1, :] * x_charged
    y_charged = y_rows[0] * neutral
    base = EXT_Y * CX
    for x in range(3):
        plane[base + x * HALO_ROWS : base + (x + 1) * HALO_ROWS, :] = (
            x_rows[0, CX + x : CX + x + 1, :] * y_charged
        )
    top = base + 3 * HALO_ROWS
    plane[top:, :] = jnp.zeros((PLANE - top, atoms), jnp.float32)
    spread = dot(z_rows[...], plane[...], (1, 1))
    tables[0].wait()
    field_out[...] = dot(fz[...], spread, (1, 0)).reshape(field_out.shape)

    def exchange(source, target, send, recv):
        def copy(o):
            p = lax.rem(me + o, n)
            return pltpu.make_async_remote_copy(
                source.at[p], target.at[me], send.at[o], recv.at[o],
                device_id=coords(p), device_id_type=MESH,
            )

        @pl.loop(1, n)
        def _(o):
            copy(o).start()

        target[me] = source[me]

        @pl.loop(1, n)
        def _(o):
            copy(o).wait()

    exchange(field_out, field_in, field_send, field_recv)

    @pl.loop(1, n)
    def _(o):
        inf_copy(o).wait()

    own_inf.wait()
    for table in tables[1:]:
        table.wait()

    low = dot(field_in[...].reshape(PLANE, PLANE), gather[...], (0, 0))
    real, imag = low[:, :NZ], low[:, NZ:]
    cosine, sine = twiddle[0], twiddle[1]
    turned = jnp.concatenate(
        [real * cosine + imag * sine, imag * cosine - real * sine], axis=0
    )
    spectrum = dot(inner[...], turned, (1, 0))
    parts = []
    for k in range(2):
        both = kernel_in[k * n // 2 : k * n // 2 + rows] + kernel_in[k * n // 2 + rows : (k + 1) * n // 2]
        parts.append(both.reshape(LANES, LANES))
    green = jnp.concatenate(parts, axis=1)
    filtered = spectrum * jnp.concatenate([green, green], axis=0)
    back = dot(inner_t[...], filtered, (1, 0))
    real, imag = back[:PLANE], back[PLANE:]
    turned = jnp.concatenate(
        [real * cosine - imag * sine, imag * cosine + real * sine], axis=1
    )
    back_out[...] = dot(gather[...], turned, (1, 1)).reshape(back_out.shape)
    exchange(back_out, back_in, back_send, back_recv)

    scale = 1.0 / float(CX * rows * CY * cols * NZ)
    potential = dot(back_in[...].reshape(PLANE, PLANE), fz[...] * scale, (0, 0))
    sampled[0] = dot(potential[:top], z_rows[...], (1, 0))
    sampled[1] = dot(potential[:top], z_slopes[...], (1, 0))
    width = 256
    for k in range(atoms // width):
        cut = slice(k * width, (k + 1) * width)
        by_y = by_dy = by_yz = 0.0
        for y in range(EXT_Y):
            row = slice(y * CX, (y + 1) * CX)
            weight = y_rows[0, y : y + 1, cut]
            by_y = by_y + weight * sampled[0, row, cut]
            by_dy = by_dy + y_rows[1, y : y + 1, cut] * sampled[0, row, cut]
            by_yz = by_yz + weight * sampled[1, row, cut]
        by_x = by_dx = by_xz = 0.0
        for x in range(3):
            row = slice(base + x * HALO_ROWS, base + (x + 1) * HALO_ROWS)
            weight = x_rows[0, CX + x : CX + x + 1, cut]
            by_x = by_x + weight * sampled[0, row, cut]
            by_dx = by_dx + x_rows[1, CX + x : CX + x + 1, cut] * sampled[0, row, cut]
            by_xz = by_xz + weight * sampled[1, row, cut]
        xs, dxs = x_rows[0, :CX, cut], x_rows[1, :CX, cut]
        ys, dys = y_rows[0, :, cut], y_rows[1, :, cut]

        def down(values):
            return jnp.sum(values, axis=0, keepdims=True)

        value = down(xs * by_y) + down(ys * by_x)
        grad_x = down(dxs * by_y) + down(ys * by_dx)
        grad_y = down(xs * by_dy) + down(dys * by_x)
        grad_z = down(xs * by_yz) + down(ys * by_xz)
        part = neutral[:, cut]
        energy_ref[:, cut] = 0.5 * part * value
        forces_ref[0:1, cut] = -part * grad_x
        forces_ref[1:2, cut] = -part * grad_y
        forces_ref[2:3, cut] = -part * grad_z


def fast_body(plan, charges, structure_id, live_count, cell_index, fraction, influence):
    rows, cols, offsets = plan
    n = rows * cols
    atoms = charges.shape[0]
    per_col = NZ // cols // n
    high = CY // rows
    stored = influence.reshape(per_col, n, high, cols, CX, rows)
    stored = stored.transpose(1, 2, 4, 0, 3, 5).reshape(n, high * CX, per_col * n)
    empty = jnp.zeros_like(stored)
    stored = jnp.where(
        lax.axis_index("col") % 2 == 0,
        jnp.concatenate([stored, empty], axis=2),
        jnp.concatenate([empty, stored], axis=2),
    )
    tables = make_tables(rows, cols)
    vmem = pl.BlockSpec(memory_space=pltpu.VMEM)
    anywhere = pl.BlockSpec(memory_space=pl.ANY)
    f32 = jnp.float32
    lines = NZ // n
    count = len(offsets)
    sems = pltpu.SemaphoreType.DMA
    forces, energy = pl.pallas_call(
        functools.partial(kernel, plan),
        out_shape=(
            jax.ShapeDtypeStruct((3, atoms), f32),
            jax.ShapeDtypeStruct((1, atoms), f32),
        ),
        in_specs=[vmem] * 5 + [anywhere] * 6,
        out_specs=(vmem, vmem),
        scratch_shapes=[
            pltpu.VMEM((NZ, NZ), f32),
            pltpu.VMEM(tables[1].shape[1:], f32),
            pltpu.VMEM(tables[2].shape, f32),
            pltpu.VMEM(tables[3].shape, f32),
            pltpu.VMEM(tables[4].shape, f32),
            pltpu.VMEM((NZ, atoms), f32),
            pltpu.VMEM((NZ, atoms), f32),
            pltpu.VMEM((PLANE, atoms), f32),
            pltpu.VMEM((2, 16, atoms), f32),
            pltpu.VMEM((2, HALO_ROWS, atoms), f32),
            pltpu.VMEM((count, 2 * S_DEV, LANES), f32),
            pltpu.VMEM((count, 2 * S_DEV, LANES), f32),
            pltpu.VMEM((S_DEV, LANES), f32),
            pltpu.VMEM((count, S_DEV, LANES), f32),
            pltpu.VMEM((n, high * CX, LANES), f32),
            pltpu.VMEM((n, lines, PLANE), f32),
            pltpu.VMEM((n, lines, PLANE), f32),
            pltpu.VMEM((n, lines, PLANE), f32),
            pltpu.VMEM((n, lines, PLANE), f32),
            pltpu.VMEM((2, EXT_Y * CX + 3 * HALO_ROWS, atoms), f32),
            sems((5,)),
            sems((count,)), sems((count,)), sems((count,)), sems((count,)),
            sems((n,)), sems((n,)), sems((n,)), sems((n,)), sems((n,)), sems((n,)),
        ],
        compiler_params=pltpu.CompilerParams(
            collective_id=0, has_side_effects=True, vmem_limit_bytes=48 * 1024 * 1024
        ),
        name="ewald_step",
    )(
        charges[None, :], structure_id[None, :], live_count[None, :], cell_index, fraction, stored,
        *[jnp.asarray(t) for t in tables],
    )
    return forces, energy[0]


def solution(mesh):
    plan = make_plan(mesh.shape["row"], mesh.shape["col"])
    placed = (
        P(("row", "col")),
        P(("row", "col")),
        P(("row", "col")),
        P(None, ("row", "col")),
        P(None, ("row", "col")),
        P("col", "row", None),
    )
    return jax.shard_map(
        body if plan is None else functools.partial(fast_body, plan),
        mesh=mesh,
        in_specs=placed,
        out_specs=(P(None, ("row", "col")), P(("row", "col"))),
        check_vma=False,
    )
```

```python
import math

import functools

import jax
import jax.numpy as jnp
import numpy as np
from jax import lax
from jax.experimental import pallas as pl
from jax.experimental.pallas import tpu as pltpu
from jax.sharding import PartitionSpec as P

CX = 8
CY = 16
NZ = 256
S_DEV = 8


highest = lax.Precision.HIGHEST


def passed_along(block, axis, distance):
    devices = range(lax.axis_size(axis))
    route = [((i - distance) % len(devices), i) for i in devices]
    return lax.ppermute(block, axis, route)


def spline_weights(fraction):
    remain = 1.0 - fraction
    square = fraction * fraction
    cubic_term = square * fraction
    values = [
        remain * remain * remain / 6.0,
        (3.0 * cubic_term - 6.0 * square + 4.0) / 6.0,
        (-3.0 * cubic_term + 3.0 * square + 3.0 * fraction + 1.0) / 6.0,
        cubic_term / 6.0,
    ]
    slopes = [
        -0.5 * remain * remain,
        0.5 * (3.0 * square - 4.0 * fraction),
        0.5 * (-3.0 * square + 2.0 * fraction + 1.0),
        0.5 * square,
    ]
    return (values, slopes)


def place_weights(weights, local, width, period):
    columns = lax.broadcasted_iota(jnp.int32, (local.shape[0], width), 1)
    result = jnp.zeros((local.shape[0], width), jnp.float32)
    for offset in range(4):
        target = (local + offset) % period
        result = result + jnp.where(columns == target[:, None], weights[offset][:, None], 0.0)
    return result


def dft_tables(length):
    counter = lax.iota(jnp.int32, length)
    product = counter[:, None] * counter[None, :] % length
    angle = 2.0 * math.pi / length * product.astype(jnp.float32)
    return (jnp.cos(angle), jnp.sin(angle))


def rotate_pair(real_part, imag_part, pattern, cosine, sine, direction):
    real_cos = jnp.einsum(pattern, real_part, cosine, precision=highest)
    real_sin = jnp.einsum(pattern, real_part, sine, precision=highest)
    imag_cos = jnp.einsum(pattern, imag_part, cosine, precision=highest)
    imag_sin = jnp.einsum(pattern, imag_part, sine, precision=highest)
    return (real_cos - direction * imag_sin, imag_cos + direction * real_sin)


def body(charges, structure_id, live_count, cell_index, fraction, influence):
    atom_total = charges.shape[0]
    row_count = lax.axis_size("row")
    col_count = lax.axis_size("col")
    mesh_x = CX * row_count
    mesh_y = CY * col_count
    structures = S_DEV * row_count * col_count
    local_x = cell_index[0] - lax.axis_index("row") * CX
    local_y = cell_index[1] - lax.axis_index("col") * CY
    live = (lax.iota(jnp.int32, atom_total) < live_count[0]).astype(jnp.float32)
    wx_val, wx_slope = spline_weights(fraction[0])
    wy_val, wy_slope = spline_weights(fraction[1])
    wz_val, wz_slope = spline_weights(fraction[2])
    big_period = 4 * (CX + CY + 8)
    x_rows = place_weights(wx_val, local_x, CX + 3, big_period)
    x_slope_rows = place_weights(wx_slope, local_x, CX + 3, big_period)
    y_rows = place_weights(wy_val, local_y, CY + 3, big_period)
    y_slope_rows = place_weights(wy_slope, local_y, CY + 3, big_period)
    z_rows = place_weights(wz_val, cell_index[2], NZ, NZ)
    z_slope_rows = place_weights(wz_slope, cell_index[2], NZ, NZ)
    plane = (y_rows[:, :, None] * x_rows[:, None, :]).reshape(atom_total, -1)
    charge_sums = jax.ops.segment_sum(charges * live, structure_id, num_segments=structures)
    live_sums = jax.ops.segment_sum(live, structure_id, num_segments=structures)
    totals, counts = lax.psum((charge_sums, live_sums), ("row", "col"))
    neutral = (charges - jnp.take(totals / counts, structure_id)) * live
    spread_grid = lax.dot_general(
        plane,
        neutral[:, None] * z_rows,
        (((0,), (0,)), ((), ())),
        precision=highest,
        preferred_element_type=jnp.float32,
    )
    extended = spread_grid.reshape(CY + 3, CX + 3, NZ)
    spill_x = passed_along(extended[:, CX:, :], "row", 1)
    extended = extended[:, :CX, :].at[:, :3, :].add(spill_x)
    spill_y = passed_along(extended[CY:], "col", 1)
    density = extended[:CY].at[:3].add(spill_y)
    cos_z, sin_z = dft_tables(NZ)
    cos_y, sin_y = dft_tables(mesh_y)
    cos_x, sin_x = dft_tables(mesh_x)
    real_z = jnp.einsum("yxz,zk->kxy", density, cos_z, precision=highest)
    imag_z = -jnp.einsum("yxz,zk->kxy", density, sin_z, precision=highest)
    columns = lax.all_to_all(
        jnp.stack([real_z, imag_z]), "col", split_axis=1, concat_axis=3, tiled=True
    )
    real_y, imag_y = rotate_pair(columns[0], columns[1], "zxy,yk->zkx", cos_y, sin_y, -1.0)
    rows = lax.all_to_all(
        jnp.stack([real_y, imag_y]), "row", split_axis=2, concat_axis=3, tiled=True
    )
    real_x, imag_x = rotate_pair(rows[0], rows[1], "zyx,xk->zyk", cos_x, sin_x, -1.0)
    scale = influence / float(mesh_x * mesh_y * NZ)
    real_x = real_x * scale
    imag_x = imag_x * scale
    back_x, back_x_imag = rotate_pair(real_x, imag_x, "zyk,kx->zyx", cos_x, sin_x, 1.0)
    returned = lax.all_to_all(
        jnp.stack([back_x, back_x_imag]), "row", split_axis=3, concat_axis=2, tiled=True
    )
    back_y, back_y_imag = rotate_pair(returned[0], returned[1], "zkx,ky->zxy", cos_y, sin_y, 1.0)
    whole_z = lax.all_to_all(
        jnp.stack([back_y, back_y_imag]), "col", split_axis=3, concat_axis=1, tiled=True
    )
    potential = jnp.einsum("kxy,kz->yxz", whole_z[0], cos_z, precision=highest) - jnp.einsum(
        "kxy,kz->yxz", whole_z[1], sin_z, precision=highest
    )
    upper_x = passed_along(potential[:, :3, :], "row", -1)
    widened = jnp.concatenate([potential, upper_x], axis=1)
    upper_y = passed_along(widened[:3], "col", -1)
    widened = jnp.concatenate([widened, upper_y], axis=0).reshape(-1, NZ)
    sampled = lax.dot_general(
        jnp.concatenate([z_rows, z_slope_rows], axis=0),
        widened,
        (((1,), (1,)), ((), ())),
        precision=highest,
        preferred_element_type=jnp.float32,
    )
    sample_val = sampled[:atom_total]
    sample_slope = sampled[atom_total:]
    plane_dx = (y_rows[:, :, None] * x_slope_rows[:, None, :]).reshape(atom_total, -1)
    plane_dy = (y_slope_rows[:, :, None] * x_rows[:, None, :]).reshape(atom_total, -1)
    value = jnp.sum(plane * sample_val, axis=1)
    grad_x = jnp.sum(plane_dx * sample_val, axis=1)
    grad_y = jnp.sum(plane_dy * sample_val, axis=1)
    grad_z = jnp.sum(plane * sample_slope, axis=1)
    atom_energy = 0.5 * neutral * value
    forces = -neutral[None, :] * jnp.stack([grad_x, grad_y, grad_z])
    return (forces, atom_energy)


EXT_Y = CY + 3
HALO_ROWS = 24
PLANE = 256
LANES = 128
MESH = pl.DeviceIdType.MESH


def plane_cells():
    cells = np.zeros((PLANE, 2), np.int64)
    used = np.zeros((PLANE,), bool)
    for y in range(EXT_Y):
        for x in range(CX):
            cells[y * CX + x] = (x, y)
            used[y * CX + x] = True
    for x in range(3):
        for y in range(EXT_Y):
            cells[EXT_Y * CX + x * HALO_ROWS + y] = (CX + x, y)
            used[EXT_Y * CX + x * HALO_ROWS + y] = True
    return cells, used


def make_plan(rows, cols):
    n = rows * cols
    offsets = [(0, 0), (1, 0), (-1, 0), (0, 1), (0, -1), (rows // 2, 0)]
    distinct = len({(a % rows, b % cols) for a, b in offsets}) == len(offsets)
    if not (
        rows % 2 == 0
        and cols % 2 == 0
        and distinct
        and NZ % (2 * n) == 0
        and (NZ // n) % 8 == 0
        and NZ % (cols * n) == 0
        and (CY * cols) % rows == 0
        and CY == 2 * rows
        and NZ // cols == 2 * n
        and (NZ // n) * n == PLANE
        and NZ // n // 2 * n == LANES
    ):
        return None
    return (rows, cols, tuple(offsets))


def make_tables(rows, cols):
    n = rows * cols
    half = NZ // n // 2
    slots = 2 * half
    z = np.arange(NZ)
    forward_z = np.zeros((n, 2, half, NZ))
    for p in range(n):
        for j in range(half):
            angle = 2 * np.pi * ((p + n * j) * z % NZ) / NZ
            forward_z[p, 0, j] = np.cos(angle)
            forward_z[p, 1, j] = -np.sin(angle)
    forward_z[0, 1, 0] = 1.0 - 2.0 * (z % 2)
    forward_z = forward_z.reshape(NZ, NZ)

    r, c, m1, k1 = np.meshgrid(
        np.arange(rows), np.arange(cols), np.arange(cols), np.arange(rows), indexing="ij"
    )
    phi = 2 * np.pi * ((k1 * r % rows) / rows + (m1 * c % cols) / cols)
    phi = phi.reshape(n, n)
    cosp, sinp = np.cos(phi), np.sin(phi)
    gather = np.zeros((2, n, 2, half, 2, slots, n))
    for kind in range(2):
        for t in range(slots):
            j, sign = t, 1.0
            if t >= half:
                j, sign = (slots - 1 - t if kind else slots - t), -1.0
            if kind == 0 and t in (0, half):
                part = 0 if t == 0 else 1
                gather[kind, :, part, 0, 0, t] = cosp
                gather[kind, :, part, 0, 1, t] = -sinp
                continue
            gather[kind, :, 0, j, 0, t] = cosp
            gather[kind, :, 1, j, 0, t] = sign * sinp
            gather[kind, :, 0, j, 1, t] = -sinp
            gather[kind, :, 1, j, 1, t] = sign * cosp
    gather = gather.reshape(2, n * 2 * half, 2 * slots * n)

    cells, used = plane_cells()
    x, y = cells[:, 0], cells[:, 1]
    low_m, low_k = (v.reshape(-1) for v in np.meshgrid(np.arange(cols), np.arange(rows), indexing="ij"))
    psi = 2 * np.pi * (
        x[:, None] * low_k[None] / (CX * rows) + y[:, None] * low_m[None] / (CY * cols)
    )
    twiddle = np.stack([np.tile(np.cos(psi), (1, slots)), np.tile(np.sin(psi), (1, slots))])
    high_m, high_k = (v.reshape(-1) for v in np.meshgrid(np.arange(CY), np.arange(CX), indexing="ij"))
    per_row = CY // rows
    order = np.arange(CY * CX).reshape(rows, per_row, CX).transpose(1, 0, 2).reshape(-1)
    high_m, high_k = high_m[order], high_k[order]
    chi = 2 * np.pi * (high_k[:, None] * x[None] % CX / CX + high_m[:, None] * y[None] % CY / CY)
    cosc, sinc = np.cos(chi) * used[None], np.sin(chi) * used[None]
    inner = np.block([[cosc, sinc], [-sinc, cosc]])
    tables = (forward_z, gather, twiddle, inner, inner.T)
    pairs = []
    for table in tables:
        table = np.asarray(table, np.float32)
        high = table.astype(jnp.bfloat16)
        low = (table - high.astype(np.float32)).astype(jnp.bfloat16)
        pairs.append(np.stack([high, low], axis=-3))
    pairs[2] = tables[2].astype(np.float32)
    return tuple(pairs)


def split(values):
    high = values.astype(jnp.bfloat16)
    return high, (values - high.astype(jnp.float32)).astype(jnp.bfloat16)


def dot(left, right, contract):
    def one(a, b):
        return lax.dot_general(
            a, b, ((contract[:1], contract[1:]), ((), ())), preferred_element_type=jnp.float32
        )

    return one(left[0], right[0]) + (one(left[0], right[1]) + one(left[1], right[0]))


def pick(distance, weights):
    result = jnp.where(distance == 3, weights[3], 0.0)
    for i in (2, 1, 0):
        result = jnp.where(distance == i, weights[i], result)
    return result


def kernel(
    plan,
    charges_ref, sid_ref, live_ref, cell_ref, frac_ref, influence_ref,
    fz_hbm, gather_hbm, twiddle_hbm, inner_hbm, inner_t_hbm,
    forces_ref, energy_ref,
    fz, gather, twiddle, inner, inner_t,
    z_rows, z_slopes, plane, x_rows, y_rows,
    frag_out, frag_in, mean_out, mean_in,
    kernel_in, field_out, field_in, back_out, back_in, sampled,
    table_sems, frag_send, frag_recv, mean_send, mean_recv,
    inf_send, inf_recv, field_send, field_recv, back_send, back_recv,
):
    rows, cols, offsets = plan
    n = rows * cols
    r, c = lax.axis_index("row"), lax.axis_index("col")
    me = r * cols + c
    atoms = charges_ref.shape[1]

    def coords(p):
        return (lax.div(p, cols), lax.rem(p, cols))

    barrier = pltpu.get_barrier_semaphore()

    @pl.loop(1, n, unroll=True)
    def _(o):
        pl.semaphore_signal(
            barrier, inc=1, device_id=coords(lax.rem(me + o, n)), device_id_type=MESH
        )

    tables = [
        pltpu.make_async_copy(fz_hbm, fz, table_sems.at[0]),
        pltpu.make_async_copy(gather_hbm.at[jnp.minimum(me, 1)], gather, table_sems.at[1]),
        pltpu.make_async_copy(twiddle_hbm, twiddle, table_sems.at[2]),
        pltpu.make_async_copy(inner_hbm, inner, table_sems.at[3]),
        pltpu.make_async_copy(inner_t_hbm, inner_t, table_sems.at[4]),
    ]
    for table in tables:
        table.start()

    lane = lax.broadcasted_iota(jnp.int32, (1, atoms), 1)
    live = (lane < live_ref[...]).astype(jnp.float32)
    charges = charges_ref[...]
    charged = charges * live
    sid = sid_ref[...]
    within = lax.broadcasted_iota(jnp.int32, (S_DEV, atoms), 0)
    steps = [
        (lax.rem(r + a % rows, rows), lax.rem(c + b % cols, cols)) for a, b in offsets
    ]
    senders = [
        (lax.rem(r + (-a) % rows, rows), lax.rem(c + (-b) % cols, cols)) for a, b in offsets
    ]

    def belongs(o):
        owner = steps[o][0] * cols + steps[o][1]
        return sid == within + owner * S_DEV

    def folded(values):
        total = values[:, :LANES]
        for k in range(1, atoms // LANES):
            total = total + values[:, k * LANES : (k + 1) * LANES]
        return total

    for o in range(len(offsets)):
        mine = belongs(o)
        frag_out[o, :S_DEV] = folded(jnp.where(mine, charged, 0.0))
        frag_out[o, S_DEV:] = folded(jnp.where(mine, live, 0.0))
    pl.semaphore_wait(barrier, n - 1)
    first = [
        pltpu.make_async_remote_copy(
            frag_out.at[o], frag_in.at[o], frag_send.at[o], frag_recv.at[o],
            device_id=steps[o], device_id_type=MESH,
        )
        for o in range(1, len(offsets))
    ]
    for copy in first:
        copy.start()

    place = c * rows + r

    def inf_copy(o):
        p = lax.rem(me + o, n)
        residue = jnp.where(c < cols // 2, p, lax.rem(n - p, n))
        return pltpu.make_async_remote_copy(
            influence_ref.at[residue], kernel_in.at[place], inf_send.at[o], inf_recv.at[o],
            device_id=coords(p), device_id_type=MESH,
        )

    @pl.loop(1, n, unroll=True)
    def _(o):
        inf_copy(o).start()

    own_inf = pltpu.make_async_copy(
        influence_ref.at[jnp.where(c < cols // 2, me, lax.rem(n - me, n))],
        kernel_in.at[place],
        inf_recv.at[0],
    )
    own_inf.start()

    wx, vx = spline_weights(frac_ref[0:1, :])
    wy, vy = spline_weights(frac_ref[1:2, :])
    wz, vz = spline_weights(frac_ref[2:3, :])
    cell_z = cell_ref[2:3, :]
    step = 16

    @pl.loop(0, NZ // step)
    def _(b):
        start = pl.multiple_of(b * step, step)
        index = lax.broadcasted_iota(jnp.int32, (step, atoms), 0) + start - cell_z
        distance = jnp.where(index < 0, index + NZ, index)
        z_rows[0, pl.ds(start, step), :], z_rows[1, pl.ds(start, step), :] = split(
            pick(distance, wz)
        )

    distance = lax.broadcasted_iota(jnp.int32, (16, atoms), 0) - (cell_ref[0:1, :] - r * CX)
    x_rows[0] = pick(distance, wx)
    x_rows[1] = pick(distance, vx)
    distance = lax.broadcasted_iota(jnp.int32, (HALO_ROWS, atoms), 0) - (
        cell_ref[1:2, :] - c * CY
    )
    y_rows[0] = pick(distance, wy)
    y_rows[1] = pick(distance, vy)

    for copy in first:
        copy.wait()
    total = frag_out[0]
    for o in range(1, len(offsets)):
        total = total + frag_in[o]
    charge_sum = jnp.sum(total[:S_DEV], axis=1, keepdims=True)
    live_sum = jnp.sum(total[S_DEV:], axis=1, keepdims=True)
    own_mean = charge_sum / live_sum
    mean_out[...] = jnp.broadcast_to(own_mean, (S_DEV, LANES))
    second = [
        pltpu.make_async_remote_copy(
            mean_out, mean_in.at[o], mean_send.at[o], mean_recv.at[o],
            device_id=senders[o], device_id_type=MESH,
        )
        for o in range(1, len(offsets))
    ]
    for copy in second:
        copy.start()

    @pl.loop(0, NZ // step)
    def _(b):
        start = pl.multiple_of(b * step, step)
        index = lax.broadcasted_iota(jnp.int32, (step, atoms), 0) + start - cell_z
        distance = jnp.where(index < 0, index + NZ, index)
        z_slopes[0, pl.ds(start, step), :], z_slopes[1, pl.ds(start, step), :] = split(
            pick(distance, vz)
        )

    for copy in second:
        copy.wait()
    mean = jnp.where(belongs(0), own_mean, 0.0)
    for o in range(1, len(offsets)):
        mean = mean + jnp.where(belongs(o), mean_in[o][:, 0:1], 0.0)
    mean = jnp.sum(mean, axis=0, keepdims=True)
    neutral = (charges - mean) * live

    x_charged = x_rows[0, :CX] * neutral
    for y in range(EXT_Y):
        plane[y * CX : (y + 1) * CX, :] = y_rows[0, y : y + 1, :] * x_charged
    y_charged = y_rows[0] * neutral
    base = EXT_Y * CX
    for x in range(3):
        plane[base + x * HALO_ROWS : base + (x + 1) * HALO_ROWS, :] = (
            x_rows[0, CX + x : CX + x + 1, :] * y_charged
        )
    top = base + 3 * HALO_ROWS
    plane[top:, :] = jnp.zeros((PLANE - top, atoms), jnp.float32)
    spread = dot((z_rows[0], z_rows[1]), split(plane[...]), (1, 1))
    tables[0].wait()
    field_out[...] = dot((fz[0], fz[1]), split(spread), (1, 0)).reshape(field_out.shape)

    def exchange(source, target, send, recv):
        def copy(o):
            p = lax.rem(me + o, n)
            return pltpu.make_async_remote_copy(
                source.at[p], target.at[me], send.at[o], recv.at[o],
                device_id=coords(p), device_id_type=MESH,
            )

        @pl.loop(1, n, unroll=True)
        def _(o):
            copy(o).start()

        target[me] = source[me]

        @pl.loop(1, n, unroll=True)
        def _(o):
            pltpu.make_async_remote_copy(
                source.at[0], target.at[0], send.at[o], recv.at[o],
                device_id=(r, c), device_id_type=MESH,
            ).wait()

    exchange(field_out, field_in, field_send, field_recv)

    @pl.loop(1, n, unroll=True)
    def _(o):
        pltpu.make_async_remote_copy(
            influence_ref.at[0], kernel_in.at[0], inf_send.at[o], inf_recv.at[o],
            device_id=(r, c), device_id_type=MESH,
        ).wait()

    own_inf.wait()
    for table in tables[1:]:
        table.wait()

    low = dot(split(field_in[...].reshape(PLANE, PLANE).T), (gather[0], gather[1]), (1, 0))
    real, imag = low[:, :NZ], low[:, NZ:]
    cosine, sine = twiddle[0], twiddle[1]
    turned = jnp.concatenate(
        [real * cosine + imag * sine, imag * cosine - real * sine], axis=0
    )
    spectrum = dot((inner[0], inner[1]), split(turned), (1, 0))
    by_col = kernel_in[...].reshape(cols, rows * CX, LANES)
    swapped = [pltpu.roll(by_col[k], LANES // 2, 1) for k in range(cols)]
    first_half = lax.broadcasted_iota(jnp.int32, (rows * CX, LANES), 1) < LANES // 2
    lower = [jnp.where(first_half, by_col[k], swapped[k + 1]) for k in range(0, cols, 2)]
    upper = [jnp.where(first_half, swapped[k], by_col[k + 1]) for k in range(0, cols, 2)]
    green = jnp.concatenate(
        [jnp.concatenate(lower, axis=1), jnp.concatenate(upper, axis=1)], axis=0
    )
    filtered = spectrum * jnp.concatenate([green, green], axis=0)
    back = dot((inner_t[0], inner_t[1]), split(filtered), (1, 0))
    real, imag = back[:PLANE], back[PLANE:]
    turned = jnp.concatenate(
        [real * cosine - imag * sine, imag * cosine + real * sine], axis=1
    )
    back_out[...] = dot((gather[0], gather[1]), split(turned), (1, 1)).reshape(back_out.shape)
    exchange(back_out, back_in, back_send, back_recv)

    scale = 1.0 / float(CX * rows * CY * cols * NZ)
    potential = dot(split(back_in[...].reshape(PLANE, PLANE).T), (fz[0], fz[1]), (1, 0))
    potential = split(potential[:top] * scale)
    sampled[0] = dot(potential, (z_rows[0], z_rows[1]), (1, 0))
    sampled[1] = dot(potential, (z_slopes[0], z_slopes[1]), (1, 0))
    width = 256
    for k in range(atoms // width):
        cut = slice(k * width, (k + 1) * width)
        by_y = by_dy = by_yz = 0.0
        for y in range(EXT_Y):
            row = slice(y * CX, (y + 1) * CX)
            weight = y_rows[0, y : y + 1, cut]
            by_y = by_y + weight * sampled[0, row, cut]
            by_dy = by_dy + y_rows[1, y : y + 1, cut] * sampled[0, row, cut]
            by_yz = by_yz + weight * sampled[1, row, cut]
        by_x = by_dx = by_xz = 0.0
        for x in range(3):
            row = slice(base + x * HALO_ROWS, base + (x + 1) * HALO_ROWS)
            weight = x_rows[0, CX + x : CX + x + 1, cut]
            by_x = by_x + weight * sampled[0, row, cut]
            by_dx = by_dx + x_rows[1, CX + x : CX + x + 1, cut] * sampled[0, row, cut]
            by_xz = by_xz + weight * sampled[1, row, cut]
        xs, dxs = x_rows[0, :CX, cut], x_rows[1, :CX, cut]
        ys, dys = y_rows[0, :, cut], y_rows[1, :, cut]

        def down(values):
            return jnp.sum(values, axis=0, keepdims=True)

        value = down(xs * by_y) + down(ys * by_x)
        grad_x = down(dxs * by_y) + down(ys * by_dx)
        grad_y = down(xs * by_dy) + down(dys * by_x)
        grad_z = down(xs * by_yz) + down(ys * by_xz)
        part = neutral[:, cut]
        energy_ref[:, cut] = 0.5 * part * value
        forces_ref[0:1, cut] = -part * grad_x
        forces_ref[1:2, cut] = -part * grad_y
        forces_ref[2:3, cut] = -part * grad_z


def fast_body(plan, charges, structure_id, live_count, cell_index, fraction, influence):
    rows, cols, offsets = plan
    n = rows * cols
    atoms = charges.shape[0]
    per_col = NZ // cols // n
    high = CY // rows
    stored = influence.reshape(per_col, n, high, cols, CX, rows)
    stored = stored.transpose(1, 4, 2, 0, 3, 5).reshape(n, CX, high * per_col * n)
    tables = make_tables(rows, cols)
    vmem = pl.BlockSpec(memory_space=pltpu.VMEM)
    anywhere = pl.BlockSpec(memory_space=pltpu.HBM)
    f32 = jnp.float32
    lines = NZ // n
    count = len(offsets)
    sems = pltpu.SemaphoreType.DMA
    forces, energy = pl.pallas_call(
        functools.partial(kernel, plan),
        out_shape=(
            jax.ShapeDtypeStruct((3, atoms), f32),
            jax.ShapeDtypeStruct((1, atoms), f32),
        ),
        in_specs=[vmem] * 5 + [anywhere] * 6,
        out_specs=(vmem, vmem),
        scratch_shapes=[
            pltpu.VMEM(tables[0].shape, jnp.bfloat16),
            pltpu.VMEM(tables[1].shape[1:], jnp.bfloat16),
            pltpu.VMEM(tables[2].shape, f32),
            pltpu.VMEM(tables[3].shape, jnp.bfloat16),
            pltpu.VMEM(tables[4].shape, jnp.bfloat16),
            pltpu.VMEM((2, NZ, atoms), jnp.bfloat16),
            pltpu.VMEM((2, NZ, atoms), jnp.bfloat16),
            pltpu.VMEM((PLANE, atoms), f32),
            pltpu.VMEM((2, 16, atoms), f32),
            pltpu.VMEM((2, HALO_ROWS, atoms), f32),
            pltpu.VMEM((count, 2 * S_DEV, LANES), f32),
            pltpu.VMEM((count, 2 * S_DEV, LANES), f32),
            pltpu.VMEM((S_DEV, LANES), f32),
            pltpu.VMEM((count, S_DEV, LANES), f32),
            pltpu.VMEM((n, CX, LANES), f32),
            pltpu.VMEM((n, lines, PLANE), f32),
            pltpu.VMEM((n, lines, PLANE), f32),
            pltpu.VMEM((n, lines, PLANE), f32),
            pltpu.VMEM((n, lines, PLANE), f32),
            pltpu.VMEM((2, EXT_Y * CX + 3 * HALO_ROWS, atoms), f32),
            sems((5,)),
            sems((count,)), sems((count,)), sems((count,)), sems((count,)),
            sems((n,)), sems((n,)), sems((n,)), sems((n,)), sems((n,)), sems((n,)),
        ],
        compiler_params=pltpu.CompilerParams(
            collective_id=0, has_side_effects=True, vmem_limit_bytes=48 * 1024 * 1024
        ),
        name="ewald_step",
    )(
        charges[None, :], structure_id[None, :], live_count[None, :], cell_index, fraction, stored,
        *[jnp.asarray(t) for t in tables],
    )
    return forces, energy[0]


def solution(mesh):
    plan = make_plan(mesh.shape["row"], mesh.shape["col"])
    placed = (
        P(("row", "col")),
        P(("row", "col")),
        P(("row", "col")),
        P(None, ("row", "col")),
        P(None, ("row", "col")),
        P("col", "row", None),
    )
    return jax.shard_map(
        body if plan is None else functools.partial(fast_body, plan),
        mesh=mesh,
        in_specs=placed,
        out_specs=(P(None, ("row", "col")), P(("row", "col"))),
        check_vma=False,
    )
```
